32 devices in a mesh: mem: 4 (over y, x), tt: 8 (over z, core).
Axes of the slice: x: 2, y: 2, z: 4, core: 2. Of those that a mesh axis runs over, the one named last changes fastest.
Arguments:
- history: bfloat16 [2, 16, 128, 16, 128], P(None, 'mem', None, 'tt'), may hold values from -0.125 to 0.125
- free_rows: bfloat16 [2, 2, 128, 16, 128], P(None, None, None, 'tt'), may hold values from -3 to 3
- memory_start: int32 [2], replicated, may hold values from 0 to 7, as said below
- now: int32 [1], replicated, may hold values from 8 to 14
Outputs:
- new_rows: bfloat16 [2, 2, 128, 16, 128], P(None, None, None, 'tt')
The draws below stay inside these ranges and needn't reach their ends.
Inputs may be any that keep to these rules, and one draw needn't show every extreme that they name: Row r's memory integral starts at memory_start[r]; starts need not be distinct, and some row starts at the largest allowed value. The new rows' times now + r lie inside the grid.
All inputs are finite; a program needn't handle non-finite values.
Results may differ from the reference program's by a relative error of at most 0.012.
The reference program's roundings to bfloat16 on the way count: a program that leaves them out, or rounds other values in their place, can miss the bound.
Values may be sent and summed in bfloat16 or wider, within the bound.
No kernel may reach another device: no remote copies, remote signals or barrier semaphores. Data moves between devices by JAX's collectives and lax.ppermute only.
A program may use at most 64 MiB of HBM per device.

```python
import jax
import jax.numpy as jnp

NORB = 128
ROWS = 2
ITERS = 3
NT = 16


def draw_memory_start(key, part):
    half = NT // 2
    value_key = jax.random.fold_in(key, 11)
    place_key = jax.random.fold_in(key, 23)
    values = jax.random.randint(value_key, (ROWS,), 0, half, dtype=jnp.int32)
    chosen = jax.random.randint(place_key, (), 0, ROWS, dtype=jnp.int32)
    positions = jnp.arange(ROWS, dtype=jnp.int32)
    values = jnp.where(positions == chosen, jnp.int32(half - 1), values)
    return values.astype(jnp.int32)


def block_scale(stream_key, extent, split, least, top_value):
    loudness, own = 1.0, jax.random.fold_in(stream_key, 6)
    for axis_at, parts in split:
        heights = jnp.exp(jax.random.uniform(jax.random.fold_in(own, axis_at), (parts,), jnp.float32, least / len(split), top_value / len(split)))
        loudness = loudness * jnp.repeat(heights, extent[axis_at] // parts).reshape([-1 if axis == axis_at else 1 for axis in range(len(extent))])
    return loudness


def normal_values(key, dims, scale, bound, split=(), held_as=jnp.bfloat16):
    array = scale * jax.random.normal(key, dims, jnp.float32)
    if split:
        array = array * block_scale(key, dims, split, -0.22, 0.18)
    return jnp.clip(array, -bound, bound).astype(held_as)


def setup_inputs(seed: int = 0) -> dict:
    seeds = jax.random.split(jax.random.key(seed), 5)
    return {
        "history": normal_values(seeds[0], (2, NT, NORB, NT, NORB), (NT * NORB) ** -0.5, 0.125, ((1, 4), (3, 8))),
        "free_rows": normal_values(seeds[1], (2, ROWS, NORB, NT, NORB), 0.5, 3.0, ((3, 8),)),
        "memory_start": draw_memory_start(jax.random.fold_in(seeds[4], 71), 0),
        "now": jax.random.randint(seeds[3], (1,), NT // 2, NT - ROWS + 1).astype(jnp.int32),
    }


COUPLING = 0.5


def reference(history, free_rows, memory_start, now):
    hist_real = history[0].reshape(NT * NORB, NT * NORB)
    hist_imag = history[1].reshape(NT * NORB, NT * NORB)
    mem_times = jnp.arange(NT, dtype=jnp.int32)
    row_time = now[0] + jnp.arange(ROWS, dtype=jnp.int32)
    live_mask = (mem_times[None, :] >= memory_start[:, None]) & (mem_times[None, :] < row_time[:, None])
    live_weight = live_mask.astype(jnp.float32)[:, None, :, None]
    free_flat = free_rows.astype(jnp.float32).reshape(2, ROWS * NORB, NT * NORB)
    current = free_rows
    for sweep in range(ITERS):
        real_part = current[0].astype(jnp.float32)
        imag_part = current[1].astype(jnp.float32)
        modulus = real_part * real_part + imag_part * imag_part
        sig_real = (-(real_part * modulus) * live_weight).astype(jnp.bfloat16).reshape(ROWS * NORB, NT * NORB)
        sig_imag = (-(imag_part * modulus) * live_weight).astype(jnp.bfloat16).reshape(ROWS * NORB, NT * NORB)
        out_real = jnp.dot(sig_real, hist_real, preferred_element_type=jnp.float32) - jnp.dot(sig_imag, hist_imag, preferred_element_type=jnp.float32)
        out_imag = jnp.dot(sig_real, hist_imag, preferred_element_type=jnp.float32) + jnp.dot(sig_imag, hist_real, preferred_element_type=jnp.float32)
        summed = jnp.stack([out_real, out_imag])
        current = (free_flat + COUPLING * summed).astype(jnp.bfloat16).reshape(free_rows.shape)
    return current
```

```python
import functools

import jax
import jax.numpy as jnp
from jax import lax
from jax.experimental import pallas as pl
from jax.experimental.pallas import tpu as pltpu
from jax.sharding import PartitionSpec as P

ITERS = 3
COUPLING = 0.5


def swap(value, axis, mask):
    count = lax.axis_size(axis)
    return lax.ppermute(value, axis, [(i, i ^ mask) for i in range(count)])


def split_kernel(*refs):
    parts, out_ref, wide = refs[:-2], refs[-2], refs[-1]
    spans, rows, lanes = out_ref.shape[1], out_ref.shape[2], wide.shape[2]
    cols = out_ref.shape[3] // lanes
    at = 0
    for ref in parts:
        for p in range(ref.shape[0]):
            for s in range(spans):
                slot = at * spans + s
                wide[slot] = ref[p, s].astype(jnp.float32)
                for c in range(cols):
                    picked = wide[slot, pl.ds(c, rows, stride=cols), :]
                    out_ref[at, s, :, c * lanes : (c + 1) * lanes] = picked.astype(jnp.bfloat16)
            at += 1


def split_history(parts):
    spans, rows, cols, lanes = parts[0].shape[1:]
    merged = [p.reshape(p.shape[0], spans, rows * cols, lanes) for p in parts]
    return pl.pallas_call(
        split_kernel,
        out_shape=jax.ShapeDtypeStruct((2, spans, rows, cols * lanes), jnp.bfloat16),
        in_specs=[pl.BlockSpec(memory_space=pltpu.VMEM)] * len(merged),
        out_specs=pl.BlockSpec(memory_space=pltpu.VMEM),
        scratch_shapes=[pltpu.VMEM((2 * spans, rows * cols, lanes), jnp.float32)],
    )(*merged)


def step_kernel(n_tt, n_mem, dims, start_ref, now_ref, free_ref, *refs):
    row_count, orb_rows, cols, lanes = dims
    blocks, hists = refs[:n_tt], refs[n_tt : n_tt + n_mem]
    out_ref, wide, sig = refs[n_tt + n_mem :]
    rows = row_count * orb_rows
    tt, mem = lax.axis_index("tt"), lax.axis_index("mem")
    row_of = lax.broadcasted_iota(jnp.int32, (rows, lanes), 0) // orb_rows
    for k in range(n_tt):
        b = tt ^ k
        for p in range(2):
            wide[k, p] = blocks[k][p].astype(jnp.float32)
        for c in range(cols):
            s = b * cols + c
            weight = jnp.zeros((rows, lanes), jnp.float32)
            for r in range(row_count):
                on = (s >= start_ref[r]) & (s < now_ref[0] + r)
                weight = jnp.where(row_of == r, jnp.where(on, 1.0, 0.0), weight)
            real = wide[k, 0, pl.ds(c, rows, stride=cols), :]
            imag = wide[k, 1, pl.ds(c, rows, stride=cols), :]
            modulus = real * real + imag * imag
            at = slice(c * lanes, (c + 1) * lanes)
            sig[b, :rows, at] = (-(real * modulus) * weight).astype(jnp.bfloat16)
            sig[b, rows:, at] = (-(imag * modulus) * weight).astype(jnp.bfloat16)
    tiles = n_tt // n_mem
    by_real = jnp.zeros((2 * rows, cols * lanes), jnp.float32)
    by_imag = jnp.zeros((2 * rows, cols * lanes), jnp.float32)
    for q in range(n_mem):
        for h in range(tiles):
            left = sig[(mem ^ q) * tiles + h]
            at = slice(h * cols, (h + 1) * cols)
            h_real = hists[q][0, at].reshape(cols * lanes, cols * lanes)
            h_imag = hists[q][1, at].reshape(cols * lanes, cols * lanes)
            by_real += jnp.dot(left, h_real, preferred_element_type=jnp.float32)
            by_imag += jnp.dot(left, h_imag, preferred_element_type=jnp.float32)
    sums = (by_real[:rows] - by_imag[rows:], by_imag[:rows] + by_real[rows:])
    for p in range(2):
        for c in range(cols):
            wide[0, p, pl.ds(c, rows, stride=cols), :] = sums[p][:, c * lanes : (c + 1) * lanes]
        new = free_ref[p].astype(jnp.float32) + COUPLING * wide[0, p]
        out_ref[p] = new.astype(jnp.bfloat16)


def step(start, now, free, blocks, hists, dims):
    row_count, orb_rows, cols, lanes = dims
    rows = row_count * orb_rows
    n_tt, n_mem = len(blocks), len(hists)
    vmem, smem = pl.BlockSpec(memory_space=pltpu.VMEM), pl.BlockSpec(memory_space=pltpu.SMEM)
    return pl.pallas_call(
        functools.partial(step_kernel, n_tt, n_mem, dims),
        out_shape=jax.ShapeDtypeStruct(free.shape, jnp.bfloat16),
        in_specs=[smem, smem] + [vmem] * (1 + n_tt + n_mem),
        out_specs=vmem,
        scratch_shapes=[
            pltpu.VMEM((n_tt, 2, rows * cols, lanes), jnp.float32),
            pltpu.VMEM((n_tt, 2 * rows, cols * lanes), jnp.bfloat16),
        ],
    )(start, now, free, *blocks, *hists)


def join_kernel(row_count, *refs):
    blocks, out_ref = refs[:-1], refs[-1]
    mem = lax.axis_index("mem")
    rows = blocks[0].shape[1] // row_count
    for k, ref in enumerate(blocks):
        at = pl.ds(pl.multiple_of((mem ^ k) * rows, rows), rows)
        for p in range(2):
            for r in range(row_count):
                out_ref[p, r, at, :] = ref[p, r * rows : (r + 1) * rows, :]


def join_rows(blocks, row_count):
    rows, lanes = blocks[0].shape[1:]
    vmem = pl.BlockSpec(memory_space=pltpu.VMEM)
    return pl.pallas_call(
        functools.partial(join_kernel, row_count),
        out_shape=jax.ShapeDtypeStruct((2, row_count, len(blocks) * rows // row_count, lanes), jnp.bfloat16),
        in_specs=[vmem] * len(blocks),
        out_specs=vmem,
    )(*blocks)


def gather_history(history):
    count = lax.axis_size("mem")
    whole = {0: history}
    halves = {}
    for k in range(1, count):
        low, high = k & -k, 1 << (k.bit_length() - 1)
        if low == high:
            whole[k] = swap(history, "mem", k)
            continue

        def part(j, p):
            return whole[j][p : p + 1] if j in whole else halves[j][p]

        halves[k] = (swap(part(k ^ low, 0), "mem", low), swap(part(k ^ high, 1), "mem", high))
    return [(whole[k],) if k in whole else halves[k] for k in range(count)]


def gather_current(own):
    count = lax.axis_size("tt")
    blocks = {0: own}
    for k in reversed(range(2, count, 2)):
        blocks[k] = swap(own, "tt", k)
    for k in range(0, count, 2):
        blocks[k + 1] = swap(blocks[k], "tt", 1)
    return [blocks[k] for k in range(count)]


def on_device(history, free_rows, memory_start, now):
    n_mem = lax.axis_size("mem")
    parts, row_count, orb_count, cols, lanes = free_rows.shape
    orb_rows = orb_count // n_mem
    at = lax.axis_index("mem") * orb_rows
    free = lax.dynamic_slice_in_dim(free_rows, at, orb_rows, 2)
    free = free.reshape(parts, row_count * orb_rows * cols, lanes)
    dims = (row_count, orb_rows, cols, lanes)
    raw = gather_history(history)
    hists = [split_history(p) for p in raw]
    current = free
    for sweep in range(ITERS):
        current = step(memory_start, now, free, gather_current(current), hists, dims)
    rows = [current] + [swap(current, "mem", k) for k in range(1, n_mem)]
    return join_rows(rows, row_count).reshape(free_rows.shape)


def solution(mesh):
    return jax.shard_map(
        on_device,
        mesh=mesh,
        in_specs=(P(None, "mem", None, "tt", None), P(None, None, None, "tt", None), P(), P()),
        out_specs=P(None, None, None, "tt", None),
        check_vma=False,
    )
```

```python
import functools

import jax
import jax.numpy as jnp
from jax import lax
from jax.experimental import pallas as pl
from jax.experimental.pallas import tpu as pltpu
from jax.sharding import PartitionSpec as P


ITERS = 3
COUPLING = 0.5
VMEM_LIMIT = 20 << 20
BOTH = ("mem", "tt")


def swap(value, mem_mask, tt_mask):
    n_mem, n_tt = lax.axis_size("mem"), lax.axis_size("tt")
    pairs = [(m * n_tt + t, (m ^ mem_mask) * n_tt + (t ^ tt_mask)) for m in range(n_mem) for t in range(n_tt)]
    return lax.ppermute(value, BOTH, pairs)


def call(kernel, out_shape, args, scratch=(), smem=0, unread=0):
    spaces = [pltpu.SMEM] * smem + [pltpu.VMEM] * (len(args) - smem - unread) + [pl.ANY] * unread
    vmem = pl.BlockSpec(memory_space=pltpu.VMEM)
    many = isinstance(out_shape, list)
    return pl.pallas_call(
        kernel,
        out_shape=[jax.ShapeDtypeStruct(s, d) for s, d in out_shape] if many else jax.ShapeDtypeStruct(*out_shape),
        in_specs=[pl.BlockSpec(memory_space=s) for s in spaces],
        out_specs=[vmem] * len(out_shape) if many else vmem,
        scratch_shapes=list(scratch),
        compiler_params=pltpu.CompilerParams(vmem_limit_bytes=VMEM_LIMIT),
    )(*args)


def rows_kernel(free_ref, keep_ref, give_ref):
    mem, core = lax.axis_index("mem"), lax.axis_index("tt") % 2
    for p in range(free_ref.shape[0]):
        for r in range(free_ref.shape[1]):
            keep_ref[p, r] = free_ref[p, r, mem, core]
            give_ref[p, r] = free_ref[p, r, mem, 1 - core]


def stack_kernel(a_ref, b_ref, out_ref):
    out_ref[0] = a_ref[...]
    out_ref[1] = b_ref[...]


def cut_kernel(at, ref, *refs):
    refs[-1][0] = ref[at]


def split_kernel(n_parts, *refs):
    parts, out_ref, wide = refs[:n_parts], refs[-2], refs[-1]
    spans, rows, lanes = out_ref.shape[1], out_ref.shape[2], wide.shape[2]
    cols = out_ref.shape[3] // lanes
    at = 0
    for ref in parts:
        for p in range(ref.shape[0]):
            for s in range(spans):
                slot = at * spans + s
                wide[slot] = ref[p, s].astype(jnp.float32)
                for c in range(cols):
                    picked = wide[slot, pl.ds(c, rows, stride=cols), :]
                    out_ref[at, s, :, c * lanes : (c + 1) * lanes] = picked.astype(jnp.bfloat16)
            at += 1


def split_history(parts):
    spans, rows, cols, lanes = parts[0].shape[1:]
    merged = [p.reshape(p.shape[0], spans, rows * cols, lanes) for p in parts]
    return call(
        functools.partial(split_kernel, len(parts)),
        ((2, spans, rows, cols * lanes), jnp.bfloat16),
        merged,
        [pltpu.VMEM((2 * spans, rows * cols, lanes), jnp.float32)],
    )


def put_sigma(tile, b, dims, start_ref, now_ref, wide, sig):
    row_count, orb_rows, cols, lanes = dims
    rows = row_count * orb_rows
    row_of = lax.broadcasted_iota(jnp.int32, (rows, lanes), 0) // orb_rows
    for p in range(2):
        wide[p] = tile[p].astype(jnp.float32)
    for c in range(cols):
        s = b * cols + c
        weight = jnp.zeros((rows, lanes), jnp.float32)
        for r in range(row_count):
            on = (s >= start_ref[r]) & (s < now_ref[0] + r)
            weight = jnp.where(row_of == r, jnp.where(on, 1.0, 0.0), weight)
        real = wide[0, pl.ds(c, rows, stride=cols), :]
        imag = wide[1, pl.ds(c, rows, stride=cols), :]
        modulus = real * real + imag * imag
        at = slice(c * lanes, (c + 1) * lanes)
        sig[:rows, at] = (-(real * modulus) * weight).astype(jnp.bfloat16)
        sig[rows:, at] = (-(imag * modulus) * weight).astype(jnp.bfloat16)


def accumulate(sums, left, hist, h, cols):
    at = slice(h * cols, (h + 1) * cols)
    depth = cols * hist.shape[2]
    return tuple(
        total + jnp.dot(left, hist[p, at].reshape(depth, hist.shape[3]), preferred_element_type=jnp.float32)
        for p, total in enumerate(sums)
    )


def as_complex(sums):
    rows = sums[0].shape[0] // 2
    return sums[0][:rows] - sums[1][rows:], sums[1][:rows] + sums[0][rows:]


def update(free, value, dims, wide, p):
    row_count, orb_rows, cols, lanes = dims
    rows = row_count * orb_rows
    for c in range(cols):
        wide[p, pl.ds(c, rows, stride=cols), :] = value[:, c * lanes : (c + 1) * lanes]
    return free.astype(jnp.float32) + COUPLING * wide[p]


def integral(tiles, hists, masks, dims, start_ref, now_ref, wide, sig):
    for k, (tile, block, place) in enumerate(tiles):
        put_sigma(tile, block, dims, start_ref, now_ref, wide.at[k], sig.at[place])
    zero = jnp.zeros((2 * dims[0] * dims[1], dims[2] * dims[3]), jnp.float32)
    sums = [(zero, zero), (zero, zero)]
    for i, mask in enumerate(masks):
        for h in range(2):
            left = sig[mask * 2 + h]
            pair = (hists[i], hists[len(masks) + i])
            sums = [accumulate(t, left, hist, h, dims[2]) for t, hist in zip(sums, pair)]
    return [as_complex(t) for t in sums]


def all_tiles(blocks):
    tt = lax.axis_index("tt")
    return [(block.at[e], tt ^ (2 * k + e), tt ^ (2 * k + e)) for k, block in enumerate(blocks) for e in range(2)]


def help_kernel(dims, lent, start_ref, now_ref, tile_ref, own, pair, out_ref, wide, sig):
    core = lax.axis_index("tt") % 2
    block = lax.axis_index("mem") ^ lent
    tiles = [(tile_ref.at[e], block * 2 + (core ^ e), core ^ e) for e in range(2)]
    for e, value in enumerate(integral(tiles, (own, pair), (0,), dims, start_ref, now_ref, wide, sig)):
        for p in range(2):
            out_ref[e, p] = value[p].astype(out_ref.dtype)


def near_kernel(dims, count, near, start_ref, now_ref, *refs):
    blocks, hists, (out_ref, wide, sig) = refs[:count], refs[count:-3], refs[-3:]
    masks = [lax.axis_index("mem") ^ q for q in near]
    for e, value in enumerate(integral(all_tiles(blocks), hists, masks, dims, start_ref, now_ref, wide, sig)):
        for p in range(2):
            out_ref[e, p] = value[p]


def first_kernel(dims, free_ref, near_ref, far_ref, *refs):
    out_ref, wide = refs[-2:]
    for e in range(2):
        for p in range(2):
            value = near_ref[e, p] + far_ref[e, p].astype(jnp.float32)
            out_ref[e, p] = update(free_ref[e, p], value, dims, wide.at[e], p).astype(out_ref.dtype)


def step_kernel(dims, count, n_mem, start_ref, now_ref, free_ref, *refs):
    blocks, hists, (out_ref, wide, sig) = refs[:count], refs[count:-3], refs[-3:]
    masks = [lax.axis_index("mem") ^ q for q in range(n_mem)]
    for e, value in enumerate(integral(all_tiles(blocks), hists, masks, dims, start_ref, now_ref, wide, sig)):
        for p in range(2):
            out_ref[e, p] = update(free_ref[e, p], value[p], dims, wide.at[e], p).astype(out_ref.dtype)


def pick_kernel(wanted, *refs):
    blocks, out_ref = refs[:-1], refs[-1]
    for k, block in enumerate(blocks):
        @pl.when((lax.axis_index("tt") ^ (2 * k)) // 2 == lax.axis_index("mem") ^ wanted)
        def _():
            out_ref[...] = block[...]


def join_kernel(row_count, *refs):
    blocks, out_ref = refs[:-1], refs[-1]
    mem, core = lax.axis_index("mem"), lax.axis_index("tt") % 2
    size = out_ref.shape[4]
    for k, ref in enumerate(blocks):
        for e in range(2):
            for p in range(2):
                for r in range(row_count):
                    out_ref[p, r, mem ^ k, core ^ e] = ref[e, p, r * size : (r + 1) * size, :]


def on_device(history, free_rows, memory_start, now):
    n_mem, n_tt = lax.axis_size("mem"), lax.axis_size("tt")
    if n_tt != 2 * n_mem:
        raise ValueError("unequal split")
    parts, row_count, orb_count, cols, lanes = free_rows.shape
    orb_rows = orb_count // n_mem
    bf16, f32 = jnp.bfloat16, jnp.float32
    live = (memory_start, now)
    dims = (row_count, orb_rows // 2, cols, lanes)
    rows = row_count * orb_rows // 2
    size = orb_rows * cols // 2
    evens = range(2, n_tt, 2)

    def stack(a, b):
        return call(stack_kernel, ((2, *a.shape), bf16), [a, b])

    def gather_current(own):
        blocks = [own] + [None] * len(evens)
        for k in reversed(evens):
            blocks[k // 2] = swap(own, 0, k)
        return blocks

    def scratch(count):
        return [
            pltpu.VMEM((count, 2, rows * cols, lanes), f32),
            pltpu.VMEM((count, 2 * rows, cols * lanes), bf16),
        ]

    raw = {0: history}
    for k in range(1, n_mem):
        if k & (k - 1) == 0:
            raw[k] = swap(history, k, 0)
    relayed = {}

    def part(k, p):
        if k in raw:
            return call(functools.partial(cut_kernel, p), ((1, *history.shape[1:4], lanes), bf16), [raw[k]])
        if (k, p) not in relayed:
            bit = 1 << (k.bit_length() - 1) if p else k & -k
            relayed[k, p] = swap(part(k ^ bit, p), bit, 0)
        return relayed[k, p]

    def parts_of(k):
        return (raw[k],) if k in raw else (part(k, 0), part(k, 1))

    keep, give = call(
        rows_kernel,
        [((parts, row_count, size, lanes), bf16)] * 2,
        [free_rows.reshape(parts, row_count, n_mem, 2, size, lanes)],
    )
    keep, give = (a.reshape(parts, rows * cols, lanes) for a in (keep, give))
    free = stack(keep, swap(give, 0, 1))
    blocks = gather_current(free)

    last, helper = n_mem - 1, 1
    lent = last ^ helper
    near = tuple(range(n_mem - 1))
    picked = call(functools.partial(pick_kernel, last), (free.shape, bf16), blocks)
    lent_block = swap(picked, helper, 0)
    split, pair = {}, {}
    for k in near:
        split[k] = split_history(parts_of(k))
        pair[k] = swap(split[k], 0, 1)
    lent_sum = call(
        functools.partial(help_kernel, dims, lent),
        ((2, parts, rows, cols * lanes), bf16),
        [*live, lent_block, split[lent], pair[lent]],
        scratch(2),
        smem=2,
    )
    last_sum = swap(lent_sum, helper, 0)
    near_sum = call(
        functools.partial(near_kernel, dims, len(blocks), near),
        ((2, parts, rows, cols * lanes), f32),
        [*live, *blocks, *(split[q] for q in near), *(pair[q] for q in near)],
        scratch(n_tt),
        smem=2,
    )
    current = call(
        functools.partial(first_kernel, dims),
        (free.shape, bf16),
        [free, near_sum, last_sum],
        [pltpu.VMEM((2, parts, rows * cols, lanes), f32)],
    )
    blocks = gather_current(current)
    split[last] = split_history(parts_of(last))
    pair[last] = swap(split[last], 0, 1)
    hists = [split[k] for k in range(n_mem)] + [pair[k] for k in range(n_mem)]
    for sweep in range(1, ITERS):
        current = call(
            functools.partial(step_kernel, dims, len(blocks), n_mem),
            (free.shape, bf16),
            [*live, free, *blocks, *hists],
            scratch(n_tt),
            smem=2,
        )
        if sweep < ITERS - 1:
            blocks = gather_current(current)
    own = stack(current[0], swap(current[1], 0, 1))
    others = [None] * n_mem
    for k in reversed(range(1, n_mem)):
        others[k] = swap(own, k, 0)
    out = call(
        functools.partial(join_kernel, row_count), ((parts, row_count, n_mem, 2, size, lanes), bf16), [own] + others[1:]
    )
    return out.reshape(free_rows.shape)


def solution(mesh):
    return jax.shard_map(
        on_device,
        mesh=mesh,
        in_specs=(P(None, "mem", None, "tt", None), P(None, None, None, "tt", None), P(), P()),
        out_specs=P(None, None, None, "tt", None),
        check_vma=False,
    )
```

```python
import functools

import jax
import jax.numpy as jnp
from jax import lax
from jax.experimental import pallas as pl
from jax.experimental.pallas import tpu as pltpu
from jax.sharding import PartitionSpec as P


ITERS = 3
COUPLING = 0.5
VMEM_LIMIT = 20 << 20
BOTH = ("mem", "tt")


def swap(value, mem_mask, tt_mask):
    n_mem, n_tt = lax.axis_size("mem"), lax.axis_size("tt")
    pairs = [(m * n_tt + t, (m ^ mem_mask) * n_tt + (t ^ tt_mask)) for m in range(n_mem) for t in range(n_tt)]
    return lax.ppermute(value, BOTH, pairs)


def call(kernel, out_shape, args, scratch=(), smem=0, unread=0):
    spaces = [pltpu.SMEM] * smem + [pltpu.VMEM] * (len(args) - smem - unread) + [pl.ANY] * unread
    vmem = pl.BlockSpec(memory_space=pltpu.VMEM)
    many = isinstance(out_shape, list)
    return pl.pallas_call(
        kernel,
        out_shape=[jax.ShapeDtypeStruct(s, d) for s, d in out_shape] if many else jax.ShapeDtypeStruct(*out_shape),
        in_specs=[pl.BlockSpec(memory_space=s) for s in spaces],
        out_specs=[vmem] * len(out_shape) if many else vmem,
        scratch_shapes=list(scratch),
        compiler_params=pltpu.CompilerParams(vmem_limit_bytes=VMEM_LIMIT),
    )(*args)


def rows_kernel(free_ref, keep_ref, give_ref):
    mem, core = lax.axis_index("mem"), lax.axis_index("tt") % 2
    for p in range(free_ref.shape[0]):
        for r in range(free_ref.shape[1]):
            keep_ref[p, r] = free_ref[p, r, mem, core]
            give_ref[p, r] = free_ref[p, r, mem, 1 - core]


def stack_kernel(a_ref, b_ref, out_ref):
    out_ref[0] = a_ref[...]
    out_ref[1] = b_ref[...]


def cut_kernel(at, ref, *refs):
    refs[-1][0] = ref[at]


def split_kernel(n_parts, *refs):
    parts, out_ref, wide = refs[:n_parts], refs[-2], refs[-1]
    spans, rows, lanes = out_ref.shape[1], out_ref.shape[2], wide.shape[2]
    cols = out_ref.shape[3] // lanes
    at = 0
    for ref in parts:
        for p in range(ref.shape[0]):
            for s in range(spans):
                slot = at * spans + s
                wide[slot] = ref[p, s].astype(jnp.float32)
                for c in range(cols):
                    picked = wide[slot, pl.ds(c, rows, stride=cols), :]
                    out_ref[at, s, :, c * lanes : (c + 1) * lanes] = picked.astype(jnp.bfloat16)
            at += 1


def split_history(parts):
    spans, rows, cols, lanes = parts[0].shape[1:]
    merged = [p.reshape(p.shape[0], spans, rows * cols, lanes) for p in parts]
    return call(
        functools.partial(split_kernel, len(parts)),
        ((2, spans, rows, cols * lanes), jnp.bfloat16),
        merged,
        [pltpu.VMEM((2 * spans, rows * cols, lanes), jnp.float32)],
    )


def live_kernel(row_count, start_ref, now_ref, out_ref):
    times, rows, lanes = out_ref.shape
    row_of = lax.broadcasted_iota(jnp.int32, (rows, lanes), 0) // (rows // row_count)
    for s in range(times):
        weight = jnp.zeros((rows, lanes), jnp.float32)
        for r in range(row_count):
            on = (s >= start_ref[r]) & (s < now_ref[0] + r)
            weight = jnp.where(row_of == r, jnp.where(on, 1.0, 0.0), weight)
        out_ref[s] = weight


def put_sigma(tile, b, dims, live_ref, wide, sig):
    row_count, orb_rows, cols, lanes = dims
    rows = row_count * orb_rows
    for p in range(2):
        wide[p] = tile[p].astype(jnp.float32)
    for c in range(cols):
        weight = live_ref[b * cols + c]
        real = wide[0, pl.ds(c, rows, stride=cols), :]
        imag = wide[1, pl.ds(c, rows, stride=cols), :]
        modulus = real * real + imag * imag
        at = slice(c * lanes, (c + 1) * lanes)
        sig[:rows, at] = (-(real * modulus) * weight).astype(jnp.bfloat16)
        sig[rows:, at] = (-(imag * modulus) * weight).astype(jnp.bfloat16)


def accumulate(sums, left, hist, h, cols):
    at = slice(h * cols, (h + 1) * cols)
    depth = cols * hist.shape[2]
    return tuple(
        total + jnp.dot(left, hist[p, at].reshape(depth, hist.shape[3]), preferred_element_type=jnp.float32)
        for p, total in enumerate(sums)
    )


def as_complex(sums):
    rows = sums[0].shape[0] // 2
    return sums[0][:rows] - sums[1][rows:], sums[1][:rows] + sums[0][rows:]


def update(free, value, dims, wide, p):
    row_count, orb_rows, cols, lanes = dims
    rows = row_count * orb_rows
    for c in range(cols):
        wide[p, pl.ds(c, rows, stride=cols), :] = value[:, c * lanes : (c + 1) * lanes]
    return free.astype(jnp.float32) + COUPLING * wide[p]


def integral(tiles, hists, masks, dims, live_ref, wide, sig):
    for k, (tile, block, place) in enumerate(tiles):
        put_sigma(tile, block, dims, live_ref, wide.at[k], sig.at[place])
    zero = jnp.zeros((2 * dims[0] * dims[1], dims[2] * dims[3]), jnp.float32)
    sums = [(zero, zero), (zero, zero)]
    for i, mask in enumerate(masks):
        for h in range(2):
            left = sig[mask * 2 + h]
            pair = (hists[i], hists[len(masks) + i])
            sums = [accumulate(t, left, hist, h, dims[2]) for t, hist in zip(sums, pair)]
    return [as_complex(t) for t in sums]


def all_tiles(blocks):
    tt = lax.axis_index("tt")
    return [(block.at[e], tt ^ (2 * k + e), tt ^ (2 * k + e)) for k, block in enumerate(blocks) for e in range(2)]


def help_kernel(dims, lent, live_ref, tile_ref, own, pair, out_ref, wide, sig):
    core = lax.axis_index("tt") % 2
    block = lax.axis_index("mem") ^ lent
    tiles = [(tile_ref.at[e], block * 2 + (core ^ e), core ^ e) for e in range(2)]
    for e, value in enumerate(integral(tiles, (own, pair), (0,), dims, live_ref, wide, sig)):
        for p in range(2):
            out_ref[e, p] = value[p].astype(out_ref.dtype)


def near_kernel(dims, count, near, live_ref, *refs):
    blocks, hists, (out_ref, wide, sig) = refs[:count], refs[count:-3], refs[-3:]
    masks = [lax.axis_index("mem") ^ q for q in near]
    for e, value in enumerate(integral(all_tiles(blocks), hists, masks, dims, live_ref, wide, sig)):
        for p in range(2):
            out_ref[e, p] = value[p]


def first_kernel(dims, free_ref, near_ref, far_ref, *refs):
    out_ref, wide = refs[-2:]
    for e in range(2):
        for p in range(2):
            value = near_ref[e, p] + far_ref[e, p].astype(jnp.float32)
            out_ref[e, p] = update(free_ref[e, p], value, dims, wide.at[e], p).astype(out_ref.dtype)


def step_kernel(dims, count, n_mem, live_ref, free_ref, *refs):
    blocks, hists, (out_ref, wide, sig) = refs[:count], refs[count:-3], refs[-3:]
    masks = [lax.axis_index("mem") ^ q for q in range(n_mem)]
    for e, value in enumerate(integral(all_tiles(blocks), hists, masks, dims, live_ref, wide, sig)):
        for p in range(2):
            out_ref[e, p] = update(free_ref[e, p], value[p], dims, wide.at[e], p).astype(out_ref.dtype)


def pick_kernel(wanted, *refs):
    blocks, out_ref = refs[:-1], refs[-1]
    for k, block in enumerate(blocks):
        @pl.when((lax.axis_index("tt") ^ (2 * k)) // 2 == lax.axis_index("mem") ^ wanted)
        def _():
            out_ref[...] = block[...]


def join_kernel(row_count, *refs):
    blocks, out_ref = refs[:-1], refs[-1]
    mem, core = lax.axis_index("mem"), lax.axis_index("tt") % 2
    size = out_ref.shape[4]
    for k, ref in enumerate(blocks):
        for e in range(2):
            for p in range(2):
                for r in range(row_count):
                    out_ref[p, r, mem ^ k, core ^ e] = ref[e, p, r * size : (r + 1) * size, :]


def on_device(history, free_rows, memory_start, now):
    n_mem, n_tt = lax.axis_size("mem"), lax.axis_size("tt")
    if n_tt != 2 * n_mem:
        raise ValueError("unequal split")
    parts, row_count, orb_count, cols, lanes = free_rows.shape
    spans = history.shape[1]
    orb_rows = orb_count // n_mem
    bf16, f32 = jnp.bfloat16, jnp.float32
    dims = (row_count, orb_rows // 2, cols, lanes)
    rows = row_count * orb_rows // 2
    size = orb_rows * cols // 2
    evens = range(2, n_tt, 2)

    def stack(a, b):
        return call(stack_kernel, ((2, *a.shape), bf16), [a, b])

    def gather_current(own):
        blocks = [own] + [None] * len(evens)
        for k in reversed(evens):
            blocks[k // 2] = swap(own, 0, k)
        return blocks

    def scratch(count):
        return [
            pltpu.VMEM((count, 2, rows * cols, lanes), f32),
            pltpu.VMEM((count, 2 * rows, cols * lanes), bf16),
        ]

    raw = {0: history}
    for k in range(1, n_mem):
        if k & (k - 1) == 0:
            raw[k] = swap(history, k, 0)
    relayed = {}

    def part(k, p):
        if k in raw:
            return call(functools.partial(cut_kernel, p), ((1, *history.shape[1:4], lanes), bf16), [raw[k]])
        if (k, p) not in relayed:
            bit = 1 << (k.bit_length() - 1) if p else k & -k
            relayed[k, p] = swap(part(k ^ bit, p), bit, 0)
        return relayed[k, p]

    def parts_of(k):
        return (raw[k],) if k in raw else (part(k, 0), part(k, 1))

    keep, give = call(
        rows_kernel,
        [((parts, row_count, size, lanes), bf16)] * 2,
        [free_rows.reshape(parts, row_count, n_mem, 2, size, lanes)],
    )
    keep, give = (a.reshape(parts, rows * cols, lanes) for a in (keep, give))
    free = stack(keep, swap(give, 0, 1))
    blocks = gather_current(free)
    live = call(
        functools.partial(live_kernel, row_count), ((spans * n_mem, rows, lanes), f32), [memory_start, now], smem=2
    )

    last, helper = n_mem - 1, 1
    lent = last ^ helper
    near = tuple(range(n_mem - 1))
    picked = call(functools.partial(pick_kernel, last), (free.shape, bf16), blocks)
    lent_block = swap(picked, helper, 0)
    split, pair = {}, {}
    for k in near:
        split[k] = split_history(parts_of(k))
        pair[k] = swap(split[k], 0, 1)
    lent_sum = call(
        functools.partial(help_kernel, dims, lent),
        ((2, parts, rows, cols * lanes), bf16),
        [live, lent_block, split[lent], pair[lent]],
        scratch(2),
    )
    last_sum = swap(lent_sum, helper, 0)
    near_sum = call(
        functools.partial(near_kernel, dims, len(blocks), near),
        ((2, parts, rows, cols * lanes), f32),
        [live, *blocks, *(split[q] for q in near), *(pair[q] for q in near)],
        scratch(n_tt),
    )
    current = call(
        functools.partial(first_kernel, dims),
        (free.shape, bf16),
        [free, near_sum, last_sum],
        [pltpu.VMEM((2, parts, rows * cols, lanes), f32)],
    )
    blocks = gather_current(current)
    split[last] = split_history(parts_of(last))
    pair[last] = swap(split[last], 0, 1)
    hists = [split[k] for k in range(n_mem)] + [pair[k] for k in range(n_mem)]
    for sweep in range(1, ITERS):
        current = call(
            functools.partial(step_kernel, dims, len(blocks), n_mem),
            (free.shape, bf16),
            [live, free, *blocks, *hists],
            scratch(n_tt),
        )
        if sweep < ITERS - 1:
            blocks = gather_current(current)
    own = stack(current[0], swap(current[1], 0, 1))
    others = [None] * n_mem
    for k in reversed(range(1, n_mem)):
        others[k] = swap(own, k, 0)
    out = call(
        functools.partial(join_kernel, row_count), ((parts, row_count, n_mem, 2, size, lanes), bf16), [own] + others[1:]
    )
    return out.reshape(free_rows.shape)


def solution(mesh):
    return jax.shard_map(
        on_device,
        mesh=mesh,
        in_specs=(P(None, "mem", None, "tt", None), P(None, None, None, "tt", None), P(), P()),
        out_specs=P(None, None, None, "tt", None),
        check_vma=False,
    )
```

```python
import functools

import jax
import jax.numpy as jnp
from jax import lax
from jax.experimental import pallas as pl
from jax.experimental.pallas import tpu as pltpu
from jax.sharding import PartitionSpec as P


ITERS = 3
COUPLING = 0.5
VMEM_LIMIT = 40 << 20
BOTH = ("mem", "tt")


def swap(value, mem_mask, tt_mask):
    n_mem, n_tt = lax.axis_size("mem"), lax.axis_size("tt")
    pairs = [(m * n_tt + t, (m ^ mem_mask) * n_tt + (t ^ tt_mask)) for m in range(n_mem) for t in range(n_tt)]
    return lax.ppermute(value, BOTH, pairs)


def call(kernel, out_shape, args, scratch=(), smem=0, unread=0):
    spaces = [pltpu.SMEM] * smem + [pltpu.VMEM] * (len(args) - smem - unread) + [pl.ANY] * unread
    vmem = pl.BlockSpec(memory_space=pltpu.VMEM)
    many = isinstance(out_shape, list)
    return pl.pallas_call(
        kernel,
        out_shape=[jax.ShapeDtypeStruct(s, d) for s, d in out_shape] if many else jax.ShapeDtypeStruct(*out_shape),
        in_specs=[pl.BlockSpec(memory_space=s) for s in spaces],
        out_specs=[vmem] * len(out_shape) if many else vmem,
        scratch_shapes=list(scratch),
        compiler_params=pltpu.CompilerParams(vmem_limit_bytes=VMEM_LIMIT),
    )(*args)


def stack_kernel(a_ref, b_ref, out_ref):
    out_ref[0] = a_ref[...]
    out_ref[1] = b_ref[...]


def cut_kernel(at, ref, *refs):
    refs[-1][0] = ref[at]


def split_kernel(n_parts, *refs):
    parts, out_ref, wide = refs[:n_parts], refs[-2], refs[-1]
    spans, rows, lanes = out_ref.shape[1], out_ref.shape[2], wide.shape[2]
    cols = out_ref.shape[3] // lanes
    at = 0
    for ref in parts:
        for p in range(ref.shape[0]):
            for s in range(spans):
                slot = at * spans + s
                wide[slot] = ref[p, s].astype(jnp.float32)
                for c in range(cols):
                    picked = wide[slot, pl.ds(c, rows, stride=cols), :]
                    out_ref[at, s, :, c * lanes : (c + 1) * lanes] = picked.astype(jnp.bfloat16)
            at += 1


def split_history(parts):
    spans, rows, cols, lanes = parts[0].shape[1:]
    merged = [p.reshape(p.shape[0], spans, rows * cols, lanes) for p in parts]
    return call(
        functools.partial(split_kernel, len(parts)),
        ((2, spans, rows, cols * lanes), jnp.bfloat16),
        merged,
        [pltpu.VMEM((2 * spans, rows * cols, lanes), jnp.float32)],
    )


def live_kernel(row_count, start_ref, now_ref, out_ref):
    times, rows, lanes = out_ref.shape
    row_of = lax.broadcasted_iota(jnp.int32, (rows, lanes), 0) // (rows // row_count)
    for s in range(times):
        weight = jnp.zeros((rows, lanes), jnp.float32)
        for r in range(row_count):
            on = (s >= start_ref[r]) & (s < now_ref[0] + r)
            weight = jnp.where(row_of == r, jnp.where(on, 1.0, 0.0), weight)
        out_ref[s] = weight


def put_sigma(tile, b, dims, live_ref, wide, sig):
    row_count, orb_rows, cols, lanes = dims
    rows = row_count * orb_rows
    for p in range(2):
        wide[p] = tile[p].astype(jnp.float32)
    for c in range(cols):
        weight = live_ref[b * cols + c]
        real = wide[0, pl.ds(c, rows, stride=cols), :]
        imag = wide[1, pl.ds(c, rows, stride=cols), :]
        modulus = real * real + imag * imag
        at = slice(c * lanes, (c + 1) * lanes)
        sig[:rows, at] = (-(real * modulus) * weight).astype(jnp.bfloat16)
        sig[rows:, at] = (-(imag * modulus) * weight).astype(jnp.bfloat16)


def accumulate(sums, left, hist, h, cols):
    at = slice(h * cols, (h + 1) * cols)
    depth = cols * hist.shape[2]
    return tuple(
        total + jnp.dot(left, hist[p, at].reshape(depth, hist.shape[3]), preferred_element_type=jnp.float32)
        for p, total in enumerate(sums)
    )


def as_complex(sums):
    rows = sums[0].shape[0] // 2
    return sums[0][:rows] - sums[1][rows:], sums[1][:rows] + sums[0][rows:]


def update(free, value, dims, wide, p):
    row_count, orb_rows, cols, lanes = dims
    rows = row_count * orb_rows
    for c in range(cols):
        wide[p, pl.ds(c, rows, stride=cols), :] = value[:, c * lanes : (c + 1) * lanes]
    return free.astype(jnp.float32) + COUPLING * wide[p]


def integral(tiles, hists, masks, dims, live_ref, wide, sig):
    for k, (tile, block, place) in enumerate(tiles):
        put_sigma(tile, block, dims, live_ref, wide.at[k], sig.at[place])
    zero = jnp.zeros((2 * dims[0] * dims[1], dims[2] * dims[3]), jnp.float32)
    sums = [(zero, zero), (zero, zero)]
    for i, mask in enumerate(masks):
        for h in range(2):
            left = sig[mask * 2 + h]
            pair = (hists[i], hists[len(masks) + i])
            sums = [accumulate(t, left, hist, h, dims[2]) for t, hist in zip(sums, pair)]
    return [as_complex(t) for t in sums]


def all_tiles(blocks):
    tt = lax.axis_index("tt")
    return [(block.at[e], tt ^ (2 * k + e), tt ^ (2 * k + e)) for k, block in enumerate(blocks) for e in range(2)]


def help_kernel(dims, lent, live_ref, tile_ref, own, pair, out_ref, wide, sig):
    core = lax.axis_index("tt") % 2
    block = lax.axis_index("mem") ^ lent
    tiles = [(tile_ref.at[e], block * 2 + (core ^ e), core ^ e) for e in range(2)]
    for e, value in enumerate(integral(tiles, (own, pair), (0,), dims, live_ref, wide, sig)):
        for p in range(2):
            out_ref[e, p] = value[p].astype(out_ref.dtype)


def near_kernel(dims, count, near, live_ref, *refs):
    blocks, hists, (out_ref, wide, sig) = refs[:count], refs[count:-3], refs[-3:]
    masks = [lax.axis_index("mem") ^ q for q in near]
    for e, value in enumerate(integral(all_tiles(blocks), hists, masks, dims, live_ref, wide, sig)):
        for p in range(2):
            out_ref[e, p] = value[p]


def first_kernel(dims, free_ref, near_ref, far_ref, *refs):
    out_ref, wide = refs[-2:]
    for e in range(2):
        for p in range(2):
            value = near_ref[e, p] + far_ref[e, p].astype(jnp.float32)
            out_ref[e, p] = update(free_ref[e, p], value, dims, wide.at[e], p).astype(out_ref.dtype)


def step_kernel(dims, count, n_mem, live_ref, free_ref, *refs):
    blocks, hists, (out_ref, wide, sig) = refs[:count], refs[count:-3], refs[-3:]
    masks = [lax.axis_index("mem") ^ q for q in range(n_mem)]
    for e, value in enumerate(integral(all_tiles(blocks), hists, masks, dims, live_ref, wide, sig)):
        for p in range(2):
            out_ref[e, p] = update(free_ref[e, p], value[p], dims, wide.at[e], p).astype(out_ref.dtype)


def collect_kernel(*refs):
    hists, out_ref = refs[:-1], refs[-1]
    count = len(hists) // 2
    for e in range(2):
        for k in range(count):
            out_ref[e, lax.axis_index("mem") ^ k] = hists[e * count + k][...]


def block_integral(sums, block, k, pairs, dims, live_ref, hist_ref, wide, sig):
    tt = lax.axis_index("tt")
    chip, core = (tt // 2) ^ k, tt % 2
    cols = dims[2]
    for e in range(2):
        h = core ^ e
        put_sigma(block.at[e], 2 * chip + h, dims, live_ref, wide.at[2 * k + e], sig.at[2 * k + e])
        for i, pair in enumerate(pairs):
            at = pl.ds(h * cols, cols)
            sums[i] = tuple(
                total
                + jnp.dot(
                    sig[2 * k + e],
                    hist_ref[pair, chip, p, at].reshape(cols * dims[3], cols * dims[3]),
                    preferred_element_type=jnp.float32,
                )
                for p, total in enumerate(sums[i])
            )
    return sums


def early_kernel(dims, early, live_ref, hist_ref, *refs):
    blocks, (out_ref, wide, sig) = refs[:-3], refs[-3:]
    zero = jnp.zeros((2 * dims[0] * dims[1], dims[2] * dims[3]), jnp.float32)
    sums = [(zero, zero), (zero, zero)]
    for k, block in zip(early, blocks):
        sums = block_integral(sums, block, k, (0, 1), dims, live_ref, hist_ref, wide, sig)
    for e in range(2):
        for p, value in enumerate(as_complex(sums[e])):
            out_ref[e, p] = value


def late_kernel(dims, late, pair, live_ref, hist_ref, block, sum_ref, free_ref, out_ref, wide, sig):
    zero = jnp.zeros((2 * dims[0] * dims[1], dims[2] * dims[3]), jnp.float32)
    (sums,) = block_integral([(zero, zero)], block, late, (pair,), dims, live_ref, hist_ref, wide, sig)
    for p, value in enumerate(as_complex(sums)):
        new = update(free_ref[pair, p], sum_ref[pair, p] + value, dims, wide.at[0], p)
        out_ref[p] = new.astype(out_ref.dtype)


def pick_kernel(wanted, *refs):
    blocks, out_ref = refs[:-1], refs[-1]
    for k, block in enumerate(blocks):
        @pl.when((lax.axis_index("tt") ^ (2 * k)) // 2 == lax.axis_index("mem") ^ wanted)
        def _():
            out_ref[...] = block[...]


def join_kernel(row_count, *refs):
    blocks, out_ref = refs[:-1], refs[-1]
    mem, core = lax.axis_index("mem"), lax.axis_index("tt") % 2
    size = out_ref.shape[4]
    for k, ref in enumerate(blocks):
        for e in range(2):
            for p in range(2):
                for r in range(row_count):
                    out_ref[p, r, mem ^ k, core ^ e] = ref[e, p, r * size : (r + 1) * size, :]


def on_device(history, free_rows, memory_start, now):
    n_mem, n_tt = lax.axis_size("mem"), lax.axis_size("tt")
    if n_tt != 2 * n_mem:
        raise ValueError("unequal split")
    parts, row_count, orb_count, cols, lanes = free_rows.shape
    spans = history.shape[1]
    orb_rows = orb_count // n_mem
    bf16, f32 = jnp.bfloat16, jnp.float32
    dims = (row_count, orb_rows // 2, cols, lanes)
    rows = row_count * orb_rows // 2
    size = orb_rows * cols // 2
    evens = range(2, n_tt, 2)

    def stack(a, b):
        return call(stack_kernel, ((2, *a.shape), bf16), [a, b])

    def gather_current(own):
        blocks = [own] + [None] * len(evens)
        for k in reversed(evens):
            blocks[k // 2] = swap(own, 0, k)
        return blocks

    def scratch(count):
        return [
            pltpu.VMEM((count, 2, rows * cols, lanes), f32),
            pltpu.VMEM((count, 2 * rows, cols * lanes), bf16),
        ]

    raw = {0: history}
    for k in range(1, n_mem):
        if k & (k - 1) == 0:
            raw[k] = swap(history, k, 0)
    relayed = {}

    def part(k, p):
        if k in raw:
            return call(functools.partial(cut_kernel, p), ((1, *history.shape[1:4], lanes), bf16), [raw[k]])
        if (k, p) not in relayed:
            bit = 1 << (k.bit_length() - 1) if p else k & -k
            relayed[k, p] = swap(part(k ^ bit, p), bit, 0)
        return relayed[k, p]

    def parts_of(k):
        return (raw[k],) if k in raw else (part(k, 0), part(k, 1))

    mem, core = lax.axis_index("mem"), lax.axis_index("tt") % 2
    by_core = free_rows.reshape(parts, row_count, n_mem, 2, size, lanes)
    keep, give = (
        lax.dynamic_slice(by_core, (0, 0, mem, c, 0, 0), (parts, row_count, 1, 1, size, lanes))
        for c in (core, 1 - core)
    )
    keep, give = (a.reshape(parts, rows * cols, lanes) for a in (keep, give))
    free = stack(keep, swap(give, 0, 1))
    blocks = gather_current(free)
    live = call(
        functools.partial(live_kernel, row_count), ((spans * n_mem, rows, lanes), f32), [memory_start, now], smem=2
    )

    last, helper = n_mem - 1, 1
    lent = last ^ helper
    near = tuple(range(n_mem - 1))
    picked = call(functools.partial(pick_kernel, last), (free.shape, bf16), blocks)
    lent_block = swap(picked, helper, 0)
    split, pair = {}, {}
    for k in near:
        split[k] = split_history(parts_of(k))
        pair[k] = swap(split[k], 0, 1)
    lent_sum = call(
        functools.partial(help_kernel, dims, lent),
        ((2, parts, rows, cols * lanes), bf16),
        [live, lent_block, split[lent], pair[lent]],
        scratch(2),
    )
    last_sum = swap(lent_sum, helper, 0)
    near_sum = call(
        functools.partial(near_kernel, dims, len(blocks), near),
        ((2, parts, rows, cols * lanes), f32),
        [live, *blocks, *(split[q] for q in near), *(pair[q] for q in near)],
        scratch(n_tt),
    )
    current = call(
        functools.partial(first_kernel, dims),
        (free.shape, bf16),
        [free, near_sum, last_sum],
        [pltpu.VMEM((2, parts, rows * cols, lanes), f32)],
    )
    blocks = gather_current(current)
    split[last] = split_history(parts_of(last))
    pair[last] = swap(split[last], 0, 1)
    hists = [split[k] for k in range(n_mem)] + [pair[k] for k in range(n_mem)]
    for _ in range(1, ITERS - 1):
        current = call(
            functools.partial(step_kernel, dims, len(blocks), n_mem),
            (free.shape, bf16),
            [live, free, *blocks, *hists],
            scratch(n_tt),
        )
        blocks = gather_current(current)
    late = n_tt // 4
    early = tuple(k for k in range(n_tt // 2) if k != late)
    ordered = call(collect_kernel, ((2, n_mem, *hists[0].shape), bf16), hists)
    early_sum = call(
        functools.partial(early_kernel, dims, early),
        ((2, parts, rows, cols * lanes), f32),
        [live, ordered, *(blocks[k] for k in early)],
        scratch(n_tt),
    )
    final = {}
    for e in (1, 0):
        final[e] = call(
            functools.partial(late_kernel, dims, late, e),
            (free.shape[1:], bf16),
            [live, ordered, blocks[late], early_sum, free],
            scratch(n_tt),
        )
        if e:
            swapped = swap(final[e], 0, 1)
    own = stack(final[0], swapped)
    others = [None] * n_mem
    for k in reversed(range(1, n_mem)):
        others[k] = swap(own, k, 0)
    out = call(
        functools.partial(join_kernel, row_count), ((parts, row_count, n_mem, 2, size, lanes), bf16), [own] + others[1:]
    )
    return out.reshape(free_rows.shape)


def solution(mesh):
    return jax.shard_map(
        on_device,
        mesh=mesh,
        in_specs=(P(None, "mem", None, "tt", None), P(None, None, None, "tt", None), P(), P()),
        out_specs=P(None, None, None, "tt", None),
        check_vma=False,
    )
```

```python
import functools

import jax
import jax.numpy as jnp
from jax import lax
from jax.experimental import pallas as pl
from jax.experimental.pallas import tpu as pltpu
from jax.sharding import PartitionSpec as P


ITERS = 3
COUPLING = 0.5
VMEM_LIMIT = 40 << 20
BOTH = ("mem", "tt")


def swap(value, mem_mask, tt_mask):
    n_mem, n_tt = lax.axis_size("mem"), lax.axis_size("tt")
    pairs = [(m * n_tt + t, (m ^ mem_mask) * n_tt + (t ^ tt_mask)) for m in range(n_mem) for t in range(n_tt)]
    return lax.ppermute(value, BOTH, pairs)


def call(kernel, out_shape, args, scratch=(), smem=0, unread=0):
    spaces = [pltpu.SMEM] * smem + [pltpu.VMEM] * (len(args) - smem - unread) + [pl.ANY] * unread
    vmem = pl.BlockSpec(memory_space=pltpu.VMEM)
    many = isinstance(out_shape, list)
    return pl.pallas_call(
        kernel,
        out_shape=[jax.ShapeDtypeStruct(s, d) for s, d in out_shape] if many else jax.ShapeDtypeStruct(*out_shape),
        in_specs=[pl.BlockSpec(memory_space=s) for s in spaces],
        out_specs=[vmem] * len(out_shape) if many else vmem,
        scratch_shapes=list(scratch),
        compiler_params=pltpu.CompilerParams(vmem_limit_bytes=VMEM_LIMIT),
    )(*args)


def stack_kernel(a_ref, b_ref, out_ref):
    out_ref[0] = a_ref[...]
    out_ref[1] = b_ref[...]


def cut_kernel(at, ref, *refs):
    refs[-1][0] = ref[at]


def split_kernel(n_parts, *refs):
    parts, out_ref, wide = refs[:n_parts], refs[-2], refs[-1]
    spans, rows, lanes = out_ref.shape[1], out_ref.shape[2], wide.shape[2]
    cols = out_ref.shape[3] // lanes
    at = 0
    for ref in parts:
        for p in range(ref.shape[0]):
            for s in range(spans):
                slot = at * spans + s
                wide[slot] = ref[p, s].astype(jnp.float32)
                for c in range(cols):
                    picked = wide[slot, pl.ds(c, rows, stride=cols), :]
                    out_ref[at, s, :, c * lanes : (c + 1) * lanes] = picked.astype(jnp.bfloat16)
            at += 1


def split_history(parts):
    spans, rows, cols, lanes = parts[0].shape[1:]
    merged = [p.reshape(p.shape[0], spans, rows * cols, lanes) for p in parts]
    return call(
        functools.partial(split_kernel, len(parts)),
        ((2, spans, rows, cols * lanes), jnp.bfloat16),
        merged,
        [pltpu.VMEM((2 * spans, rows * cols, lanes), jnp.float32)],
    )


def live_kernel(row_count, start_ref, now_ref, out_ref):
    times, rows, lanes = out_ref.shape
    row_of = lax.broadcasted_iota(jnp.int32, (rows, lanes), 0) // (rows // row_count)
    for s in range(times):
        weight = jnp.zeros((rows, lanes), jnp.float32)
        for r in range(row_count):
            on = (s >= start_ref[r]) & (s < now_ref[0] + r)
            weight = jnp.where(row_of == r, jnp.where(on, 1.0, 0.0), weight)
        out_ref[s] = weight


def put_sigma(tile, b, dims, live_ref, wide, sig, scale=None):
    row_count, orb_rows, cols, lanes = dims
    rows = row_count * orb_rows
    for p in range(2):
        wide[p] = tile[p].astype(jnp.float32)
    for c in range(cols):
        weight = live_ref[b * cols + c]
        if scale is not None:
            weight = weight * scale
        real = wide[0, pl.ds(c, rows, stride=cols), :]
        imag = wide[1, pl.ds(c, rows, stride=cols), :]
        modulus = real * real + imag * imag
        at = slice(c * lanes, (c + 1) * lanes)
        sig[:rows, at] = (-(real * modulus) * weight).astype(jnp.bfloat16)
        sig[rows:, at] = (-(imag * modulus) * weight).astype(jnp.bfloat16)


def accumulate(sums, left, hist, h, cols):
    at = slice(h * cols, (h + 1) * cols)
    depth = cols * hist.shape[2]
    return tuple(
        total + jnp.dot(left, hist[p, at].reshape(depth, hist.shape[3]), preferred_element_type=jnp.float32)
        for p, total in enumerate(sums)
    )


def as_complex(sums):
    rows = sums[0].shape[0] // 2
    return sums[0][:rows] - sums[1][rows:], sums[1][:rows] + sums[0][rows:]


def update(free, value, dims, wide, p):
    row_count, orb_rows, cols, lanes = dims
    rows = row_count * orb_rows
    for c in range(cols):
        wide[p, pl.ds(c, rows, stride=cols), :] = value[:, c * lanes : (c + 1) * lanes]
    return free.astype(jnp.float32) + COUPLING * wide[p]


def integral(tiles, hists, masks, dims, live_ref, wide, sig):
    for k, (tile, block, place) in enumerate(tiles):
        put_sigma(tile, block, dims, live_ref, wide.at[k], sig.at[place])
    zero = jnp.zeros((2 * dims[0] * dims[1], dims[2] * dims[3]), jnp.float32)
    sums = [(zero, zero), (zero, zero)]
    for i, mask in enumerate(masks):
        for h in range(2):
            left = sig[mask * 2 + h]
            pair = (hists[i], hists[len(masks) + i])
            sums = [accumulate(t, left, hist, h, dims[2]) for t, hist in zip(sums, pair)]
    return [as_complex(t) for t in sums]


def all_tiles(blocks):
    tt = lax.axis_index("tt")
    return [(block.at[e], tt ^ (2 * k + e), tt ^ (2 * k + e)) for k, block in enumerate(blocks) for e in range(2)]


def help_kernel(dims, lent, live_ref, tile_ref, own, pair, out_ref, wide, sig):
    core = lax.axis_index("tt") % 2
    block = lax.axis_index("mem") ^ lent
    tiles = [(tile_ref.at[e], block * 2 + (core ^ e), core ^ e) for e in range(2)]
    for e, value in enumerate(integral(tiles, (own, pair), (0,), dims, live_ref, wide, sig)):
        for p in range(2):
            out_ref[e, p] = value[p].astype(out_ref.dtype)


def near_kernel(dims, count, near, live_ref, *refs):
    blocks, hists, (out_ref, wide, sig) = refs[:count], refs[count:-3], refs[-3:]
    masks = [lax.axis_index("mem") ^ q for q in near]
    for e, value in enumerate(integral(all_tiles(blocks), hists, masks, dims, live_ref, wide, sig)):
        for p in range(2):
            out_ref[e, p] = value[p]


def first_kernel(dims, free_ref, near_ref, far_ref, *refs):
    out_ref, wide = refs[-2:]
    for e in range(2):
        for p in range(2):
            value = near_ref[e, p] + far_ref[e, p].astype(jnp.float32)
            out_ref[e, p] = update(free_ref[e, p], value, dims, wide.at[e], p).astype(out_ref.dtype)


def collect_kernel(masks, *refs):
    hists, out_ref = refs[:-1], refs[-1]
    count = len(hists) // 2
    for e in range(2):
        for k in range(out_ref.shape[1]):
            i = masks.index(k) if k in masks else 0
            out_ref[e, lax.axis_index("mem") ^ k] = hists[e * count + i][...]


def block_integral(sums, block, k, pairs, dims, live_ref, hist_ref, wide, sig, missing=None):
    tt = lax.axis_index("tt")
    chip, core = (tt // 2) ^ k, tt % 2
    cols = dims[2]
    scale = None if missing is None else jnp.where(chip == missing, 0.0, 1.0)
    for e in range(2):
        h = core ^ e
        put_sigma(block.at[e], 2 * chip + h, dims, live_ref, wide.at[2 * k + e], sig.at[2 * k + e], scale)
        for i, pair in enumerate(pairs):
            at = pl.ds(h * cols, cols)
            sums[i] = tuple(
                total
                + jnp.dot(
                    sig[2 * k + e],
                    hist_ref[pair, chip, p, at].reshape(cols * dims[3], cols * dims[3]),
                    preferred_element_type=jnp.float32,
                )
                for p, total in enumerate(sums[i])
            )
    return sums


def early_kernel(dims, early, last, live_ref, hist_ref, *refs):
    blocks, (out_ref, wide, sig) = refs[:-3], refs[-3:]
    zero = jnp.zeros((2 * dims[0] * dims[1], dims[2] * dims[3]), jnp.float32)
    sums = [(zero, zero), (zero, zero)]
    missing = None if last is None else lax.axis_index("mem") ^ last
    for k, block in zip(early, blocks):
        sums = block_integral(sums, block, k, (0, 1), dims, live_ref, hist_ref, wide, sig, missing)
    for e in range(2):
        for p, value in enumerate(as_complex(sums[e])):
            out_ref[e, p] = value


def rest_kernel(dims, late, last, live_ref, hist_ref, own, pair, sum_ref, free_ref, *refs):
    blocks, (out_ref, wide, sig) = refs[:-3], refs[-3:]
    count = 2 * len(blocks)
    mem, tt = lax.axis_index("mem"), lax.axis_index("tt")
    missing = mem ^ last
    for k, block in enumerate(blocks):
        @pl.when((tt // 2) ^ k == missing)
        def _():
            for h in range(2):
                e = (tt % 2) ^ h
                put_sigma(block.at[e], 2 * missing + h, dims, live_ref, wide.at[count + h], sig.at[count + h])
    zero = jnp.zeros((2 * dims[0] * dims[1], dims[2] * dims[3]), jnp.float32)
    sums = [(zero, zero), (zero, zero)]
    for h in range(2):
        sums = [accumulate(t, sig[count + h], hist, h, dims[2]) for t, hist in zip(sums, (own, pair))]
    sums = block_integral(sums, blocks[late], late, (0, 1), dims, live_ref, hist_ref, wide, sig, missing)
    for e in range(2):
        for p, value in enumerate(as_complex(sums[e])):
            new = update(free_ref[e, p], sum_ref[e, p] + value, dims, wide.at[e], p)
            out_ref[e, p] = new.astype(out_ref.dtype)


def late_kernel(dims, late, pair, live_ref, hist_ref, block, sum_ref, free_ref, out_ref, wide, sig):
    zero = jnp.zeros((2 * dims[0] * dims[1], dims[2] * dims[3]), jnp.float32)
    (sums,) = block_integral([(zero, zero)], block, late, (pair,), dims, live_ref, hist_ref, wide, sig)
    for p, value in enumerate(as_complex(sums)):
        new = update(free_ref[pair, p], sum_ref[pair, p] + value, dims, wide.at[0], p)
        out_ref[p] = new.astype(out_ref.dtype)


def pick_kernel(wanted, *refs):
    blocks, out_ref = refs[:-1], refs[-1]
    for k, block in enumerate(blocks):
        @pl.when((lax.axis_index("tt") ^ (2 * k)) // 2 == lax.axis_index("mem") ^ wanted)
        def _():
            out_ref[...] = block[...]


def join_kernel(row_count, *refs):
    blocks, out_ref = refs[:-1], refs[-1]
    mem, core = lax.axis_index("mem"), lax.axis_index("tt") % 2
    size = out_ref.shape[4]
    for k, ref in enumerate(blocks):
        for e in range(2):
            for p in range(2):
                for r in range(row_count):
                    out_ref[p, r, mem ^ k, core ^ e] = ref[e, p, r * size : (r + 1) * size, :]


def on_device(history, free_rows, memory_start, now):
    n_mem, n_tt = lax.axis_size("mem"), lax.axis_size("tt")
    if n_tt != 2 * n_mem:
        raise ValueError("unequal split")
    parts, row_count, orb_count, cols, lanes = free_rows.shape
    spans = history.shape[1]
    orb_rows = orb_count // n_mem
    bf16, f32 = jnp.bfloat16, jnp.float32
    dims = (row_count, orb_rows // 2, cols, lanes)
    rows = row_count * orb_rows // 2
    size = orb_rows * cols // 2
    evens = range(2, n_tt, 2)

    def stack(a, b):
        return call(stack_kernel, ((2, *a.shape), bf16), [a, b])

    def gather_current(own):
        blocks = [own] + [None] * len(evens)
        for k in reversed(evens):
            blocks[k // 2] = swap(own, 0, k)
        return blocks

    def scratch(count):
        return [
            pltpu.VMEM((count, 2, rows * cols, lanes), f32),
            pltpu.VMEM((count, 2 * rows, cols * lanes), bf16),
        ]

    raw = {0: history}
    for k in range(1, n_mem):
        if k & (k - 1) == 0:
            raw[k] = swap(history, k, 0)
    relayed = {}

    def part(k, p):
        if k in raw:
            return call(functools.partial(cut_kernel, p), ((1, *history.shape[1:4], lanes), bf16), [raw[k]])
        if (k, p) not in relayed:
            bit = 1 << (k.bit_length() - 1) if p else k & -k
            relayed[k, p] = swap(part(k ^ bit, p), bit, 0)
        return relayed[k, p]

    def parts_of(k):
        return (raw[k],) if k in raw else (part(k, 0), part(k, 1))

    mem, core = lax.axis_index("mem"), lax.axis_index("tt") % 2
    by_core = free_rows.reshape(parts, row_count, n_mem, 2, size, lanes)
    keep, give = (
        lax.dynamic_slice(by_core, (0, 0, mem, c, 0, 0), (parts, row_count, 1, 1, size, lanes))
        for c in (core, 1 - core)
    )
    keep, give = (a.reshape(parts, rows * cols, lanes) for a in (keep, give))
    free = stack(keep, swap(give, 0, 1))
    blocks = gather_current(free)
    live = call(
        functools.partial(live_kernel, row_count), ((spans * n_mem, rows, lanes), f32), [memory_start, now], smem=2
    )

    last, helper = n_mem - 1, 1
    lent = last ^ helper
    near = tuple(range(n_mem - 1))
    picked = call(functools.partial(pick_kernel, last), (free.shape, bf16), blocks)
    lent_block = swap(picked, helper, 0)
    split, pair = {}, {}
    for k in near:
        split[k] = split_history(parts_of(k))
        pair[k] = swap(split[k], 0, 1)
    lent_sum = call(
        functools.partial(help_kernel, dims, lent),
        ((2, parts, rows, cols * lanes), bf16),
        [live, lent_block, split[lent], pair[lent]],
        scratch(2),
    )
    last_sum = swap(lent_sum, helper, 0)
    near_sum = call(
        functools.partial(near_kernel, dims, len(blocks), near),
        ((2, parts, rows, cols * lanes), f32),
        [live, *blocks, *(split[q] for q in near), *(pair[q] for q in near)],
        scratch(n_tt),
    )
    current = call(
        functools.partial(first_kernel, dims),
        (free.shape, bf16),
        [free, near_sum, last_sum],
        [pltpu.VMEM((2, parts, rows * cols, lanes), f32)],
    )
    blocks = gather_current(current)
    split[last] = split_history(parts_of(last))
    pair[last] = swap(split[last], 0, 1)
    late = n_tt // 4
    early = tuple(k for k in range(n_tt // 2) if k != late)

    def collect(masks):
        shape = (2, n_mem, *split[0].shape)
        picked = [h[k] for h in (split, pair) for k in masks]
        return call(functools.partial(collect_kernel, masks), (shape, bf16), picked)

    some = collect(near)
    for _ in range(1, ITERS - 1):
        early_sum = call(
            functools.partial(early_kernel, dims, early, last),
            ((2, parts, rows, cols * lanes), f32),
            [live, some, *(blocks[k] for k in early)],
            scratch(n_tt),
        )
        current = call(
            functools.partial(rest_kernel, dims, late, last),
            (free.shape, bf16),
            [live, some, split[last], pair[last], early_sum, free, *blocks],
            scratch(n_tt + 2),
        )
        blocks = gather_current(current)
    ordered = collect(tuple(range(n_mem)))
    early_sum = call(
        functools.partial(early_kernel, dims, early, None),
        ((2, parts, rows, cols * lanes), f32),
        [live, ordered, *(blocks[k] for k in early)],
        scratch(n_tt),
    )
    final = {}
    for e in (1, 0):
        final[e] = call(
            functools.partial(late_kernel, dims, late, e),
            (free.shape[1:], bf16),
            [live, ordered, blocks[late], early_sum, free],
            scratch(n_tt),
        )
        if e:
            swapped = swap(final[e], 0, 1)
    own = stack(final[0], swapped)
    others = [None] * n_mem
    for k in reversed(range(1, n_mem)):
        others[k] = swap(own, k, 0)
    out = call(
        functools.partial(join_kernel, row_count), ((parts, row_count, n_mem, 2, size, lanes), bf16), [own] + others[1:]
    )
    return out.reshape(free_rows.shape)


def solution(mesh):
    return jax.shard_map(
        on_device,
        mesh=mesh,
        in_specs=(P(None, "mem", None, "tt", None), P(None, None, None, "tt", None), P(), P()),
        out_specs=P(None, None, None, "tt", None),
        check_vma=False,
    )
```
